32 devices in a mesh: groups: 2 (over y), docs: 8 (over z, x), help: 2 (over core).
Axes of the slice: x: 2, y: 2, z: 4, core: 2. Of those that a mesh axis runs over, the one named last changes fastest.
Arguments:
- token_states: bfloat16 [4096, 2, 1024], P(('groups', 'docs', 'help')), parts along dimension 0, may hold values from -6 to 6
- lengths: int32 [4096], P(('groups', 'docs', 'help')), parts along dimension 0, may hold values from 1 to 2
- cluster_id: int32 [4096], P(('groups', 'docs', 'help')), parts along dimension 0, may hold values from 0 to 7, as said below
- proj_weight: bfloat16 [1024, 1024], replicated, may hold values from -0.1875 to 0.1875
- proj_bias: float32 [1024], replicated, may hold values from -4 to 4
Outputs:
- max_sim: float32 [4096], P(('groups', 'docs', 'help')), parts along dimension 0
The draws below stay inside these ranges and needn't reach their ends.
There are 2 independent parts, one for each index of `groups`. The reference program is written for one: setup_inputs(seed, part) draws one part's arguments, and reference() takes and returns one part's arrays. A program takes and returns all parts, laid end to end along the dimension named above; an argument that names none is the same for every part. Nothing has to cross between parts.
Inputs may be any that keep to these rules, and one draw needn't show every extreme that they name: `cluster_id`: clusters 1 * k to 1 * k + 1 - 1 form owner k. Among the 128 documents of one device (aligned blocks of the document dimension), at most 32 belong to one owner, and in every draw one owner gets exactly 32 documents from every device.
All inputs are finite; a program needn't handle non-finite values.
Results may differ from the reference program's by a relative error of at most 0.0003.
Values may be sent and summed in bfloat16 or wider, within the bound.
A program may use at most 64 MiB of HBM per device.

```python
import jax
import jax.numpy as jnp
from jax import lax

D = 1024
SEQ = 2
DOC_DEV = 128
CL_OWN = 1
CAP = 32
DOCS = 2048
CLUSTERS = 8


def draw_cluster_id(key, part):
    blocks = DOCS // DOC_DEV
    owners = CLUSTERS // CL_OWN
    position_count = owners * CAP
    key_hot, key_pop, key_score, key_order, key_local = jax.random.split(key, 5)
    busiest_holder = jax.random.randint(key_hot, (), 0, owners)
    frequent_clusters = jax.random.randint(key_pop, (owners,), 0, 4)
    position_holder = jnp.arange(position_count, dtype=jnp.int32) // CAP
    extra_reward = frequent_clusters[position_holder] + jnp.where(position_holder == busiest_holder, 8, 0)
    random_jitter = jax.random.randint(key_score, (blocks, position_count), 0, 65536)
    duplicate_scores = (extra_reward[None, :] * 16384 + random_jitter) * position_count + jnp.arange(position_count, dtype=jnp.int32)[None, :]
    top_vals, chosen = lax.top_k(duplicate_scores, DOC_DEV)
    owner_rows = chosen // CAP
    shuffle_keys = jax.random.randint(key_order, (blocks, DOC_DEV), 0, 65536) * DOC_DEV + jnp.arange(DOC_DEV, dtype=jnp.int32)[None, :]
    shuffled_order = jnp.argsort(shuffle_keys, axis=1)
    owner_rows = jnp.take_along_axis(owner_rows, shuffled_order, axis=1).reshape(DOCS)
    local_idx = jax.random.randint(key_local, (DOCS,), 0, CL_OWN)
    return (owner_rows * CL_OWN + local_idx).astype(jnp.int32)


def with_ends(array, stream_key, least, top_value):
    longest = array.shape.index(max(array.shape))
    spots = []
    for shift in (0, 1):
        where = [jax.random.randint(jax.random.fold_in(stream_key, axis), (), 0, length) for axis, length in enumerate(array.shape)]
        where[longest] = (where[longest] + shift) % array.shape[longest]
        spots.append(tuple(where))
    return array.at[spots[0]].set(least).at[spots[1]].set(top_value)


def block_scale(rng, dims, cuts, low, largest):
    gain = 1.0
    for axis_at, blocks in cuts:
        heights = jax.random.uniform(jax.random.fold_in(jax.random.fold_in(rng, 6), axis_at), (blocks,), jnp.float32, low / len(cuts), largest / len(cuts))
        gain = gain * jnp.repeat(jnp.exp(heights), dims[axis_at] // blocks).reshape((-1,) + (1,) * (len(dims) - 1 - axis_at))
    return gain


def centred(own_key, dims, width, most, cuts=(), kind=jnp.bfloat16):
    entries = width * jax.random.normal(own_key, dims, jnp.float32)
    if cuts:
        entries = entries * block_scale(own_key, dims, cuts, -0.22, 0.18)
    return jnp.clip(entries, -most, most).astype(kind)


def setup_inputs(seed: int = 0, part: int = 0) -> dict:
    arg_keys = jax.random.split(jax.random.key(seed), 6)
    part_splits = jax.random.split(jax.random.fold_in(arg_keys[5], part), 6)
    return {
        "token_states": centred(part_splits[0], (DOCS, SEQ, D), 1.0, 6.0, ((0, 16),)),
        "lengths": with_ends(jax.random.randint(part_splits[1], (DOCS,), 1, SEQ + 1), jax.random.fold_in(part_splits[1], 1), 1, SEQ).astype(jnp.int32),
        "cluster_id": draw_cluster_id(jax.random.fold_in(jax.random.fold_in(arg_keys[5], part), 71), part),
        "proj_weight": centred(arg_keys[3], (D, D), D ** -0.5, 0.1875),
        "proj_bias": centred(arg_keys[4], (D,), 1.0, 4.0, (), jnp.float32),
    }


def embed_docs(token_states, lengths, proj_weight, proj_bias):
    seq_len = token_states.shape[1]
    feat_dim = token_states.shape[2]

    def embed_block(pieces):
        states, counts = pieces
        token_mask = (jnp.arange(seq_len, dtype=jnp.int32)[None, :] < counts[:, None]).astype(jnp.float32)
        summed = jnp.einsum('rsd,rs->rd', states.astype(jnp.float32), token_mask)
        pooled = (summed / counts[:, None].astype(jnp.float32)).astype(jnp.bfloat16)
        hidden = jnp.tanh(jnp.dot(pooled, proj_weight, preferred_element_type=jnp.float32) + proj_bias)
        factor = lax.rsqrt(lax.optimization_barrier(jnp.sum(hidden * hidden, axis=1, keepdims=True)) + 1e-06)
        return (hidden * factor).astype(jnp.bfloat16)
    block_count = token_states.shape[0] // DOC_DEV
    shaped = token_states.reshape(block_count, DOC_DEV, seq_len, feat_dim)
    counts = lengths.reshape(block_count, DOC_DEV)
    return lax.map(embed_block, (shaped, counts)).reshape(token_states.shape[0], feat_dim)

def reference(token_states, lengths, cluster_id, proj_weight, proj_bias):
    embedded = embed_docs(token_states, lengths, proj_weight, proj_bias)
    total = cluster_id.shape[0]
    feat_dim = embedded.shape[1]
    sort_order = jnp.argsort(cluster_id, stable=True).astype(jnp.int32)
    sorted_ids = cluster_id[sort_order]
    sorted_emb = embedded[sort_order]
    reach = 4 * DOC_DEV
    row_block = min(512, total)
    span = row_block + 2 * reach
    edge_ids = jnp.full((reach,), -2, jnp.int32)
    edge_emb = jnp.zeros((reach, feat_dim), embedded.dtype)
    pad_ids = jnp.concatenate([edge_ids, sorted_ids, edge_ids])
    pad_emb = jnp.concatenate([edge_emb, sorted_emb, edge_emb], axis=0)

    def block_max(start):
        row_emb = lax.dynamic_slice_in_dim(sorted_emb, start, row_block, 0)
        row_ids = lax.dynamic_slice_in_dim(sorted_ids, start, row_block, 0)
        col_emb = lax.dynamic_slice_in_dim(pad_emb, start, span, 0)
        col_ids = lax.dynamic_slice_in_dim(pad_ids, start, span, 0)
        duplicate_scores = jnp.einsum('rd,cd->rc', row_emb.astype(jnp.float32), col_emb.astype(jnp.float32))
        row_pos = start + jnp.arange(row_block, dtype=jnp.int32)
        col_pos = start - reach + jnp.arange(span, dtype=jnp.int32)
        match = (row_ids[:, None] == col_ids[None, :]) & (row_pos[:, None] != col_pos[None, :])
        return lax.optimization_barrier(jnp.max(jnp.where(match, duplicate_scores, -1.0), axis=1))
    starts = jnp.arange(total // row_block, dtype=jnp.int32) * row_block
    sorted_max = lax.map(block_max, starts).reshape(total)
    return jnp.zeros((total,), jnp.float32).at[sort_order].set(sorted_max)
```

```python
import functools

import jax
import jax.numpy as jnp
from jax import lax
from jax.experimental import pallas as pl
from jax.experimental.pallas import tpu as pltpu
from jax.sharding import PartitionSpec as P

CL_OWN = 1


def partner(value, axis, bit):
    return lax.ppermute(value, axis, [(i, i ^ 1 << bit) for i in range(lax.axis_size(axis))])


def slot_maxima(own_emb, own_ids, self_pos, col_emb, col_ids):
    row_total = own_emb.shape[0]
    block = min(row_total, 512)
    col_pos = lax.broadcasted_iota(jnp.int32, (col_emb.shape[0],), 0)

    def block_max(pieces):
        part_emb, part_ids, part_self = pieces
        duplicate_scores = jnp.einsum(
            "rd,cd->rc", part_emb, col_emb, preferred_element_type=jnp.float32
        )
        match = (
            (part_ids[:, None] == col_ids[None, :])
            & (col_ids[None, :] >= 0)
            & (part_self[:, None] != col_pos[None, :])
        )
        return jnp.max(jnp.where(match, duplicate_scores, -1.0), axis=1)

    steps_count = row_total // block
    result = lax.map(
        block_max,
        (
            own_emb.reshape(steps_count, block, own_emb.shape[1]),
            own_ids.reshape(steps_count, block),
            self_pos.reshape(steps_count, block),
        ),
    )
    return result.reshape(row_total)


def body(token_states, lengths, cluster_id, proj_weight, proj_bias):
    row_count, seq_len, feat_dim = token_states.shape
    owners = lax.axis_size("docs")
    slot_cap = 2 * row_count // owners
    position_count = owners * slot_cap
    token_mask = (
        lax.broadcasted_iota(jnp.int32, (row_count, seq_len), 1) < lengths[:, None]
    ).astype(jnp.bfloat16)
    summed = jnp.einsum("rsd,rs->rd", token_states, token_mask, preferred_element_type=jnp.float32)
    pooled = (summed / lengths[:, None].astype(jnp.float32)).astype(jnp.bfloat16)
    hidden = jnp.tanh(jnp.dot(pooled, proj_weight, preferred_element_type=jnp.float32) + proj_bias)
    factor = lax.rsqrt(jnp.sum(hidden * hidden, axis=1, keepdims=True) + 1e-06)
    embedded = (hidden * factor).astype(jnp.bfloat16)
    dest_owner = cluster_id // CL_OWN
    same_owner = dest_owner[:, None] == dest_owner[None, :]
    earlier = lax.broadcasted_iota(jnp.int32, (row_count, row_count), 1) < lax.broadcasted_iota(
        jnp.int32, (row_count, row_count), 0
    )
    slot_rank = jnp.sum((same_owner & earlier).astype(jnp.int32), axis=1)
    target = dest_owner * slot_cap + slot_rank
    chooser = lax.broadcasted_iota(jnp.int32, (position_count, row_count), 0) == target[None, :]
    packed = jnp.dot(
        chooser.astype(jnp.bfloat16), embedded, preferred_element_type=jnp.float32
    ).astype(jnp.bfloat16)
    packed_ids = jnp.max(jnp.where(chooser, cluster_id[None, :], -1), axis=1)
    own_emb, own_ids = (
        lax.all_to_all(packed, "docs", split_axis=0, concat_axis=0, tiled=True),
        lax.all_to_all(packed_ids, "docs", split_axis=0, concat_axis=0, tiled=True),
    )
    mate_emb, mate_ids = partner((own_emb, own_ids), "help", 0)
    col_emb = jnp.concatenate([own_emb, mate_emb], axis=0)
    col_ids = jnp.concatenate([own_ids, mate_ids], axis=0)
    self_pos = lax.broadcasted_iota(jnp.int32, (position_count,), 0)
    maxima = slot_maxima(own_emb, own_ids, self_pos, col_emb, col_ids)
    returned = lax.all_to_all(maxima, "docs", split_axis=0, concat_axis=0, tiled=True)
    return jnp.max(jnp.where(chooser, returned[:, None], -3.0), axis=0)


EMPTY = 2.0
DIRECT_LIMIT = 16


def flipped(index, step):
    bit = 1
    while bit <= step:
        if step & bit:
            index = index + bit * (1 - 2 * ((index // bit) % 2))
        bit *= 2
    return index


def send_order(owners):
    half = owners // 2
    return list(range(half, owners)) + list(range(half - 1, 0, -1))


def fused_kernel(
    owners,
    slot_cap,
    pooled_ref,
    ids_ref,
    weight_hbm,
    bias_ref,
    out_ref,
    weight_ref,
    packed_ref,
    own_ref,
    mate_ref,
    maxima_ref,
    returned_ref,
    weight_sem,
    pack_send,
    pack_recv,
    mate_send,
    mate_recv,
    back_send,
    back_recv,
):
    me = lax.axis_index("docs")
    side = lax.axis_index("help")
    mate = {"help": 1 - side}
    order = send_order(owners)
    positions = owners * slot_cap
    row_count, feat_dim = pooled_ref.shape

    weight_copy = pltpu.make_async_copy(weight_hbm, weight_ref, weight_sem)
    weight_copy.start()
    barrier = pltpu.get_barrier_semaphore()
    for step in order:
        pl.semaphore_signal(
            barrier, inc=1, device_id={"docs": flipped(me, step)}, device_id_type=pl.DeviceIdType.MESH
        )
    pl.semaphore_signal(barrier, inc=1, device_id=mate, device_id_type=pl.DeviceIdType.MESH)

    ids = ids_ref[...]
    across = jnp.broadcast_to(ids, (row_count, row_count))
    down = jnp.transpose(across)
    earlier = lax.broadcasted_iota(jnp.int32, (row_count, row_count), 0) < lax.broadcasted_iota(
        jnp.int32, (row_count, row_count), 1
    )
    rank = jnp.sum(jnp.where((across == down) & earlier, 1, 0), axis=0, keepdims=True)
    target = jnp.bitwise_xor(ids // CL_OWN, me) * slot_cap + rank

    weight_copy.wait()
    hidden = jnp.tanh(
        jnp.dot(pooled_ref[...], weight_ref[...], preferred_element_type=jnp.float32) + bias_ref[...]
    )
    factor = lax.rsqrt(jnp.sum(hidden * hidden, axis=1, keepdims=True) + 1e-06)
    embedded = (hidden * factor).astype(jnp.bfloat16)

    def pack(step):
        slots = lax.broadcasted_iota(jnp.int32, (slot_cap, row_count), 0) + step * slot_cap
        chooser = jnp.where(slots == target, 1.0, 0.0)
        filled = jnp.sum(chooser, axis=1, keepdims=True)
        rows = jnp.dot(
            chooser.astype(jnp.bfloat16), embedded, preferred_element_type=jnp.float32
        )
        return jnp.where(filled > 0.5, rows, EMPTY).astype(jnp.bfloat16)

    def to_owner(step):
        return pltpu.make_async_remote_copy(
            src_ref=packed_ref.at[step],
            dst_ref=own_ref.at[step],
            send_sem=pack_send.at[step],
            recv_sem=pack_recv.at[step],
            device_id={"docs": flipped(me, step)},
            device_id_type=pl.DeviceIdType.MESH,
        )

    def to_mate(step):
        return pltpu.make_async_remote_copy(
            src_ref=own_ref.at[step],
            dst_ref=mate_ref.at[step],
            send_sem=mate_send.at[step],
            recv_sem=mate_recv.at[step],
            device_id=mate,
            device_id_type=pl.DeviceIdType.MESH,
        )

    def to_source(step):
        return pltpu.make_async_remote_copy(
            src_ref=maxima_ref,
            dst_ref=returned_ref.at[step],
            send_sem=back_send.at[step],
            recv_sem=back_recv.at[step],
            device_id={"docs": flipped(me, step)},
            device_id_type=pl.DeviceIdType.MESH,
        )

    packed_ref[order[0]] = pack(order[0])
    pl.semaphore_wait(barrier, owners)
    to_owner(order[0]).start()
    for step in order[1:]:
        packed_ref[step] = pack(step)
        to_owner(step).start()
    own_ref[0] = pack(0)
    to_mate(0).start()
    for step in reversed(order):
        to_owner(step).wait_recv()
        to_mate(step).start()
    for step in range(owners):
        to_mate(step).wait_recv()

    own = own_ref[...].reshape(positions, feat_dim)

    def column_max(columns, exclude_self):
        scores = lax.dot_general(
            columns, own, (((1,), (1,)), ((), ())), preferred_element_type=jnp.float32
        )
        keep = columns[:, 0:1].astype(jnp.float32) < 1.5
        if exclude_self:
            keep = keep & (
                lax.broadcasted_iota(jnp.int32, (positions, positions), 0)
                != lax.broadcasted_iota(jnp.int32, (positions, positions), 1)
            )
        return jnp.max(jnp.where(keep, scores, -1.0), axis=0, keepdims=True)

    maxima = jnp.maximum(
        column_max(own, True), column_max(mate_ref[...].reshape(positions, feat_dim), False)
    )
    maxima_ref[...] = maxima
    for step in order:
        to_source(step).start()

    place = lax.broadcasted_iota(jnp.int32, (1, positions), 1) // slot_cap
    merged = jnp.where(place == 0, maxima, 0.0)
    for step in order:
        to_source(step).wait_recv()
        merged = jnp.where(place == step, returned_ref[step], merged)
    finder = jnp.where(
        lax.broadcasted_iota(jnp.int32, (positions, row_count), 0) == target, 1.0, 0.0
    )
    picked = jnp.dot(
        jnp.broadcast_to(merged, (8, positions)),
        finder,
        preferred_element_type=jnp.float32,
        precision=lax.Precision.HIGHEST,
    )
    out_ref[...] = jnp.maximum(picked[0:1], -1.0)
    for step in order:
        to_owner(step).wait_send()
        to_source(step).wait_send()
    for step in range(owners):
        to_mate(step).wait_send()


def fused_body(token_states, lengths, cluster_id, proj_weight, proj_bias):
    row_count, seq_len, feat_dim = token_states.shape
    owners = lax.axis_size("docs")
    slot_cap = 2 * row_count // owners
    positions = owners * slot_cap
    token_mask = (
        lax.broadcasted_iota(jnp.int32, (row_count, seq_len), 1) < lengths[:, None]
    ).astype(jnp.float32)
    summed = jnp.sum(token_states.astype(jnp.float32) * token_mask[:, :, None], axis=1)
    pooled = (summed / lengths[:, None].astype(jnp.float32)).astype(jnp.bfloat16)
    vmem = pl.BlockSpec(memory_space=pltpu.VMEM)
    block = (owners, slot_cap, feat_dim)
    result = pl.pallas_call(
        functools.partial(fused_kernel, owners, slot_cap),
        out_shape=jax.ShapeDtypeStruct((1, row_count), jnp.float32),
        in_specs=[vmem, vmem, pl.BlockSpec(memory_space=pl.ANY), vmem],
        out_specs=vmem,
        scratch_shapes=[
            pltpu.VMEM(proj_weight.shape, jnp.bfloat16),
            pltpu.VMEM(block, jnp.bfloat16),
            pltpu.VMEM(block, jnp.bfloat16),
            pltpu.VMEM(block, jnp.bfloat16),
            pltpu.VMEM((1, positions), jnp.float32),
            pltpu.VMEM((owners, 1, positions), jnp.float32),
            pltpu.SemaphoreType.DMA,
        ]
        + [pltpu.SemaphoreType.DMA((owners,))] * 6,
        compiler_params=pltpu.CompilerParams(collective_id=0, has_side_effects=True),
        name="scores",
    )(pooled, cluster_id[None, :], proj_weight, proj_bias[None, :])
    return result.reshape(row_count)


def solution(mesh):
    in_specs = (
        P(("groups", "docs", "help"), None, None),
        P(("groups", "docs", "help")),
        P(("groups", "docs", "help")),
        P(),
        P(),
    )
    out_specs = P(("groups", "docs", "help"))
    owners = mesh.shape["docs"]
    direct = owners <= DIRECT_LIMIT and owners & (owners - 1) == 0 and mesh.shape["help"] == 2
    return jax.shard_map(fused_body if direct else body, mesh=mesh, in_specs=in_specs, out_specs=out_specs, check_vma=False)
```

```python
import functools

import jax
import jax.numpy as jnp
from jax import lax
from jax.experimental import pallas as pl
from jax.experimental.pallas import tpu as pltpu
from jax.sharding import PartitionSpec as P

CL_OWN = 1


def partner(value, axis, bit):
    return lax.ppermute(value, axis, [(i, i ^ 1 << bit) for i in range(lax.axis_size(axis))])


def slot_maxima(own_emb, own_ids, self_pos, col_emb, col_ids):
    row_total = own_emb.shape[0]
    block = min(row_total, 512)
    col_pos = lax.broadcasted_iota(jnp.int32, (col_emb.shape[0],), 0)

    def block_max(pieces):
        part_emb, part_ids, part_self = pieces
        duplicate_scores = jnp.einsum(
            "rd,cd->rc", part_emb, col_emb, preferred_element_type=jnp.float32
        )
        match = (
            (part_ids[:, None] == col_ids[None, :])
            & (col_ids[None, :] >= 0)
            & (part_self[:, None] != col_pos[None, :])
        )
        return jnp.max(jnp.where(match, duplicate_scores, -1.0), axis=1)

    steps_count = row_total // block
    result = lax.map(
        block_max,
        (
            own_emb.reshape(steps_count, block, own_emb.shape[1]),
            own_ids.reshape(steps_count, block),
            self_pos.reshape(steps_count, block),
        ),
    )
    return result.reshape(row_total)


def body(token_states, lengths, cluster_id, proj_weight, proj_bias):
    row_count, seq_len, feat_dim = token_states.shape
    owners = lax.axis_size("docs")
    slot_cap = 2 * row_count // owners
    position_count = owners * slot_cap
    token_mask = (
        lax.broadcasted_iota(jnp.int32, (row_count, seq_len), 1) < lengths[:, None]
    ).astype(jnp.bfloat16)
    summed = jnp.einsum("rsd,rs->rd", token_states, token_mask, preferred_element_type=jnp.float32)
    pooled = (summed / lengths[:, None].astype(jnp.float32)).astype(jnp.bfloat16)
    hidden = jnp.tanh(jnp.dot(pooled, proj_weight, preferred_element_type=jnp.float32) + proj_bias)
    factor = lax.rsqrt(jnp.sum(hidden * hidden, axis=1, keepdims=True) + 1e-06)
    embedded = (hidden * factor).astype(jnp.bfloat16)
    dest_owner = cluster_id // CL_OWN
    same_owner = dest_owner[:, None] == dest_owner[None, :]
    earlier = lax.broadcasted_iota(jnp.int32, (row_count, row_count), 1) < lax.broadcasted_iota(
        jnp.int32, (row_count, row_count), 0
    )
    slot_rank = jnp.sum((same_owner & earlier).astype(jnp.int32), axis=1)
    target = dest_owner * slot_cap + slot_rank
    chooser = lax.broadcasted_iota(jnp.int32, (position_count, row_count), 0) == target[None, :]
    packed = jnp.dot(
        chooser.astype(jnp.bfloat16), embedded, preferred_element_type=jnp.float32
    ).astype(jnp.bfloat16)
    packed_ids = jnp.max(jnp.where(chooser, cluster_id[None, :], -1), axis=1)
    own_emb, own_ids = (
        lax.all_to_all(packed, "docs", split_axis=0, concat_axis=0, tiled=True),
        lax.all_to_all(packed_ids, "docs", split_axis=0, concat_axis=0, tiled=True),
    )
    mate_emb, mate_ids = partner((own_emb, own_ids), "help", 0)
    col_emb = jnp.concatenate([own_emb, mate_emb], axis=0)
    col_ids = jnp.concatenate([own_ids, mate_ids], axis=0)
    self_pos = lax.broadcasted_iota(jnp.int32, (position_count,), 0)
    maxima = slot_maxima(own_emb, own_ids, self_pos, col_emb, col_ids)
    returned = lax.all_to_all(maxima, "docs", split_axis=0, concat_axis=0, tiled=True)
    return jnp.max(jnp.where(chooser, returned[:, None], -3.0), axis=0)


EMPTY = 2.0
DIRECT_LIMIT = 16


def flipped(index, step):
    bit = 1
    while bit <= step:
        if step & bit:
            index = index + bit * (1 - 2 * ((index // bit) % 2))
        bit *= 2
    return index


def send_order(owners):
    half = owners // 2
    return list(range(half, owners)) + list(range(half - 1, 0, -1))


def fused_kernel(
    owners,
    slot_cap,
    states_ref,
    lengths_ref,
    ids_ref,
    weight_hbm,
    bias_ref,
    out_ref,
    weight_ref,
    packed_ref,
    own_ref,
    mate_ref,
    maxima_ref,
    returned_ref,
    weight_sem,
    pack_send,
    pack_recv,
    mate_send,
    mate_recv,
    back_send,
    back_recv,
):
    me = lax.axis_index("docs")
    side = lax.axis_index("help")
    mate = {"help": 1 - side}
    order = send_order(owners)
    positions = owners * slot_cap
    row_count, seq_len, feat_dim = states_ref.shape

    weight_copy = pltpu.make_async_copy(weight_hbm, weight_ref, weight_sem)
    weight_copy.start()
    barrier = pltpu.get_barrier_semaphore()
    for step in order:
        pl.semaphore_signal(
            barrier, inc=1, device_id={"docs": flipped(me, step)}, device_id_type=pl.DeviceIdType.MESH
        )
    pl.semaphore_signal(barrier, inc=1, device_id=mate, device_id_type=pl.DeviceIdType.MESH)

    ids = ids_ref[...]
    across = jnp.broadcast_to(ids, (row_count, row_count))
    down = jnp.transpose(across)
    earlier = lax.broadcasted_iota(jnp.int32, (row_count, row_count), 0) < lax.broadcasted_iota(
        jnp.int32, (row_count, row_count), 1
    )
    rank = jnp.sum(jnp.where((across == down) & earlier, 1, 0), axis=0, keepdims=True)
    target = jnp.bitwise_xor(ids // CL_OWN, me) * slot_cap + rank

    counts = jnp.transpose(jnp.broadcast_to(lengths_ref[...].astype(jnp.float32), (row_count, row_count)))[:, 0:1]
    states = states_ref[...]
    summed = states[:, 0, :].astype(jnp.float32)
    for position in range(1, seq_len):
        summed = summed + jnp.where(counts > position, states[:, position, :].astype(jnp.float32), 0.0)
    pooled = (summed / counts).astype(jnp.bfloat16)

    weight_copy.wait()
    hidden = jnp.tanh(
        jnp.dot(pooled, weight_ref[...], preferred_element_type=jnp.float32) + bias_ref[...]
    )
    factor = lax.rsqrt(jnp.sum(hidden * hidden, axis=1, keepdims=True) + 1e-06)
    embedded = (hidden * factor).astype(jnp.bfloat16)

    def pack(step):
        slots = lax.broadcasted_iota(jnp.int32, (slot_cap, row_count), 0) + step * slot_cap
        chooser = jnp.where(slots == target, 1.0, 0.0)
        filled = jnp.sum(chooser, axis=1, keepdims=True)
        rows = jnp.dot(
            chooser.astype(jnp.bfloat16), embedded, preferred_element_type=jnp.float32
        )
        return jnp.where(filled > 0.5, rows, EMPTY).astype(jnp.bfloat16)

    def to_owner(step):
        return pltpu.make_async_remote_copy(
            src_ref=packed_ref.at[step],
            dst_ref=own_ref.at[step],
            send_sem=pack_send.at[step],
            recv_sem=pack_recv.at[step],
            device_id={"docs": flipped(me, step)},
            device_id_type=pl.DeviceIdType.MESH,
        )

    def to_mate(step):
        return pltpu.make_async_remote_copy(
            src_ref=own_ref.at[step],
            dst_ref=mate_ref.at[step],
            send_sem=mate_send.at[step],
            recv_sem=mate_recv.at[step],
            device_id=mate,
            device_id_type=pl.DeviceIdType.MESH,
        )

    def to_source(step):
        return pltpu.make_async_remote_copy(
            src_ref=maxima_ref,
            dst_ref=returned_ref.at[step],
            send_sem=back_send.at[step],
            recv_sem=back_recv.at[step],
            device_id={"docs": flipped(me, step)},
            device_id_type=pl.DeviceIdType.MESH,
        )

    packed_ref[order[0]] = pack(order[0])
    pl.semaphore_wait(barrier, owners)
    to_owner(order[0]).start()
    for step in order[1:]:
        packed_ref[step] = pack(step)
        to_owner(step).start()
    own_ref[0] = pack(0)
    to_mate(0).start()
    for step in reversed(order):
        to_owner(step).wait_recv()
        to_mate(step).start()
    for step in range(owners):
        to_mate(step).wait_recv()

    own = own_ref[...].reshape(positions, feat_dim)

    def column_max(columns, exclude_self):
        scores = lax.dot_general(
            columns, own, (((1,), (1,)), ((), ())), preferred_element_type=jnp.float32
        )
        keep = columns[:, 0:1].astype(jnp.float32) < 1.5
        if exclude_self:
            keep = keep & (
                lax.broadcasted_iota(jnp.int32, (positions, positions), 0)
                != lax.broadcasted_iota(jnp.int32, (positions, positions), 1)
            )
        return jnp.max(jnp.where(keep, scores, -1.0), axis=0, keepdims=True)

    maxima = jnp.maximum(
        column_max(own, True), column_max(mate_ref[...].reshape(positions, feat_dim), False)
    )
    maxima_ref[...] = maxima
    for step in order:
        to_source(step).start()

    place = lax.broadcasted_iota(jnp.int32, (1, positions), 1) // slot_cap
    merged = jnp.where(place == 0, maxima, 0.0)
    for step in order:
        to_source(step).wait_recv()
        merged = jnp.where(place == step, returned_ref[step], merged)
    finder = jnp.where(
        lax.broadcasted_iota(jnp.int32, (positions, row_count), 0) == target, 1.0, 0.0
    )
    picked = jnp.dot(
        jnp.broadcast_to(merged, (8, positions)),
        finder,
        preferred_element_type=jnp.float32,
        precision=lax.Precision.HIGHEST,
    )
    out_ref[...] = jnp.maximum(picked[0:1], -1.0)
    for step in order:
        to_owner(step).wait_send()
        to_source(step).wait_send()
    for step in range(owners):
        to_mate(step).wait_send()


def fused_body(token_states, lengths, cluster_id, proj_weight, proj_bias):
    row_count, seq_len, feat_dim = token_states.shape
    owners = lax.axis_size("docs")
    slot_cap = 2 * row_count // owners
    positions = owners * slot_cap
    vmem = pl.BlockSpec(memory_space=pltpu.VMEM)
    block = (owners, slot_cap, feat_dim)
    result = pl.pallas_call(
        functools.partial(fused_kernel, owners, slot_cap),
        out_shape=jax.ShapeDtypeStruct((1, row_count), jnp.float32),
        in_specs=[vmem, vmem, vmem, pl.BlockSpec(memory_space=pl.ANY), vmem],
        out_specs=vmem,
        scratch_shapes=[
            pltpu.VMEM(proj_weight.shape, jnp.bfloat16),
            pltpu.VMEM(block, jnp.bfloat16),
            pltpu.VMEM(block, jnp.bfloat16),
            pltpu.VMEM(block, jnp.bfloat16),
            pltpu.VMEM((1, positions), jnp.float32),
            pltpu.VMEM((owners, 1, positions), jnp.float32),
            pltpu.SemaphoreType.DMA,
        ]
        + [pltpu.SemaphoreType.DMA((owners,))] * 6,
        compiler_params=pltpu.CompilerParams(collective_id=0, has_side_effects=True),
        name="scores",
    )(token_states, lengths[None, :], cluster_id[None, :], proj_weight, proj_bias[None, :])
    return result.reshape(row_count)


def solution(mesh):
    in_specs = (
        P(("groups", "docs", "help"), None, None),
        P(("groups", "docs", "help")),
        P(("groups", "docs", "help")),
        P(),
        P(),
    )
    out_specs = P(("groups", "docs", "help"))
    owners = mesh.shape["docs"]
    direct = owners <= DIRECT_LIMIT and owners & (owners - 1) == 0 and mesh.shape["help"] == 2
    return jax.shard_map(fused_body if direct else body, mesh=mesh, in_specs=in_specs, out_specs=out_specs, check_vma=False)
```

```python
import functools

import jax
import jax.numpy as jnp
from jax import lax
from jax.experimental import pallas as pl
from jax.experimental.pallas import tpu as pltpu
from jax.sharding import PartitionSpec as P

CL_OWN = 1


def partner(value, axis, bit):
    return lax.ppermute(value, axis, [(i, i ^ 1 << bit) for i in range(lax.axis_size(axis))])


def slot_maxima(own_emb, own_ids, self_pos, col_emb, col_ids):
    row_total = own_emb.shape[0]
    block = min(row_total, 512)
    col_pos = lax.broadcasted_iota(jnp.int32, (col_emb.shape[0],), 0)

    def block_max(pieces):
        part_emb, part_ids, part_self = pieces
        duplicate_scores = jnp.einsum(
            "rd,cd->rc", part_emb, col_emb, preferred_element_type=jnp.float32
        )
        match = (
            (part_ids[:, None] == col_ids[None, :])
            & (col_ids[None, :] >= 0)
            & (part_self[:, None] != col_pos[None, :])
        )
        return jnp.max(jnp.where(match, duplicate_scores, -1.0), axis=1)

    steps_count = row_total // block
    result = lax.map(
        block_max,
        (
            own_emb.reshape(steps_count, block, own_emb.shape[1]),
            own_ids.reshape(steps_count, block),
            self_pos.reshape(steps_count, block),
        ),
    )
    return result.reshape(row_total)


def body(token_states, lengths, cluster_id, proj_weight, proj_bias):
    row_count, seq_len, feat_dim = token_states.shape
    owners = lax.axis_size("docs")
    slot_cap = 2 * row_count // owners
    position_count = owners * slot_cap
    token_mask = (
        lax.broadcasted_iota(jnp.int32, (row_count, seq_len), 1) < lengths[:, None]
    ).astype(jnp.bfloat16)
    summed = jnp.einsum("rsd,rs->rd", token_states, token_mask, preferred_element_type=jnp.float32)
    pooled = (summed / lengths[:, None].astype(jnp.float32)).astype(jnp.bfloat16)
    hidden = jnp.tanh(jnp.dot(pooled, proj_weight, preferred_element_type=jnp.float32) + proj_bias)
    factor = lax.rsqrt(jnp.sum(hidden * hidden, axis=1, keepdims=True) + 1e-06)
    embedded = (hidden * factor).astype(jnp.bfloat16)
    dest_owner = cluster_id // CL_OWN
    same_owner = dest_owner[:, None] == dest_owner[None, :]
    earlier = lax.broadcasted_iota(jnp.int32, (row_count, row_count), 1) < lax.broadcasted_iota(
        jnp.int32, (row_count, row_count), 0
    )
    slot_rank = jnp.sum((same_owner & earlier).astype(jnp.int32), axis=1)
    target = dest_owner * slot_cap + slot_rank
    chooser = lax.broadcasted_iota(jnp.int32, (position_count, row_count), 0) == target[None, :]
    packed = jnp.dot(
        chooser.astype(jnp.bfloat16), embedded, preferred_element_type=jnp.float32
    ).astype(jnp.bfloat16)
    packed_ids = jnp.max(jnp.where(chooser, cluster_id[None, :], -1), axis=1)
    own_emb, own_ids = (
        lax.all_to_all(packed, "docs", split_axis=0, concat_axis=0, tiled=True),
        lax.all_to_all(packed_ids, "docs", split_axis=0, concat_axis=0, tiled=True),
    )
    mate_emb, mate_ids = partner((own_emb, own_ids), "help", 0)
    col_emb = jnp.concatenate([own_emb, mate_emb], axis=0)
    col_ids = jnp.concatenate([own_ids, mate_ids], axis=0)
    self_pos = lax.broadcasted_iota(jnp.int32, (position_count,), 0)
    maxima = slot_maxima(own_emb, own_ids, self_pos, col_emb, col_ids)
    returned = lax.all_to_all(maxima, "docs", split_axis=0, concat_axis=0, tiled=True)
    return jnp.max(jnp.where(chooser, returned[:, None], -3.0), axis=0)


EMPTY = 2.0
DIRECT_LIMIT = 16


def flipped(index, step):
    bit = 1
    while bit <= step:
        if step & bit:
            index = index + bit * (1 - 2 * ((index // bit) % 2))
        bit *= 2
    return index


def fused_kernel(
    owners,
    slot_cap,
    states_hbm,
    lengths_ref,
    ids_ref,
    weight_hbm,
    bias_ref,
    out_ref,
    states_ref,
    weight_ref,
    packed_ref,
    own_ref,
    maxima_ref,
    returned_ref,
    states_sem,
    weight_sem,
    pack_send,
    pack_recv,
    back_send,
    back_recv,
    onward_sem,
):
    me = lax.axis_index("docs")
    side = lax.axis_index("help")
    row_count, seq_len, feat_dim = states_ref.shape
    quarter = owners // 4
    half = owners // 2
    sources = 2 * owners
    late = 2 * 3 * quarter
    group = row_count // slot_cap
    my_half = me // half
    near = me + my_half * (owners - 1 - 2 * me)
    outer = 1 - near // quarter
    is_owner = near >= quarter

    states_copy = pltpu.make_async_copy(states_hbm, states_ref, states_sem)
    states_copy.start()
    weight_copy = pltpu.make_async_copy(weight_hbm, weight_ref, weight_sem)
    weight_copy.start()
    barrier = pltpu.get_barrier_semaphore()
    peers = [(step, flip) for step in range(owners - 1, -1, -1) for flip in (0, 1) if step + flip]

    def peer_id(step, flip):
        return {"docs": flipped(me, step), "help": flipped(side, flip)}

    inner = [(spot, spot_side) for spot in range(quarter, half) for spot_side in (0, 1)]

    def greet(semaphore):
        def signal(spot, spot_side):
            docs = spot + my_half * (owners - 1 - 2 * spot)
            pl.semaphore_signal(
                semaphore,
                inc=1,
                device_id={"docs": docs, "help": spot_side},
                device_id_type=pl.DeviceIdType.MESH,
            )

        @pl.when(is_owner)
        def _():
            for spot, spot_side in inner:
                signal(owners - 1 - spot, spot_side)
                signal(spot - quarter, spot_side)

        @pl.when(jnp.logical_not(is_owner))
        def _():
            for spot, spot_side in inner:
                signal(spot, spot_side)

    def await_greetings(semaphore):
        pl.semaphore_wait(semaphore, len(inner) * (2 - outer))

    greet(barrier)

    ids = ids_ref[...]
    across = jnp.broadcast_to(ids, (row_count, row_count))
    down = jnp.transpose(across)
    earlier = lax.broadcasted_iota(jnp.int32, (row_count, row_count), 0) < lax.broadcasted_iota(
        jnp.int32, (row_count, row_count), 1
    )
    rank = jnp.sum(jnp.where((across == down) & earlier, 1, 0), axis=0, keepdims=True)
    dest = ids // CL_OWN

    counts = jnp.transpose(
        jnp.broadcast_to(lengths_ref[...].astype(jnp.float32), (row_count, row_count))
    )[:, 0:1]
    states_copy.wait()
    states = states_ref[...]
    summed = states[:, 0, :].astype(jnp.float32)
    for position in range(1, seq_len):
        token = states[:, position, :].astype(jnp.float32)
        summed = summed + jnp.where(counts > position, token, 0.0)
    pooled = (summed / counts).astype(jnp.bfloat16)

    weight_copy.wait()
    hidden = jnp.tanh(
        jnp.dot(pooled, weight_ref[...], preferred_element_type=jnp.float32) + bias_ref[...]
    )
    factor = lax.rsqrt(jnp.sum(hidden * hidden, axis=1, keepdims=True) + 1e-06)
    embedded = (hidden * factor).astype(jnp.bfloat16)

    def turn_target(turn):
        spot = quarter + (turn // 2 + (1 - outer) * quarter) % half
        spot_side = turn % 2
        docs = spot + my_half * (owners - 1 - 2 * spot)
        number = (docs - quarter) * 2 + spot_side
        crosses = spot // half
        slot = (near + crosses * (owners - 1 - 2 * near)) * 2 + side
        return docs, spot_side, number, slot

    def pack(number):
        slots = lax.broadcasted_iota(jnp.int32, (slot_cap, row_count), 0)
        chooser = jnp.where((slots == rank) & (dest == number), 1.0, 0.0)
        filled = jnp.sum(chooser, axis=1, keepdims=True)
        rows = jnp.dot(
            chooser.astype(jnp.bfloat16), embedded, preferred_element_type=jnp.float32
        )
        return jnp.where(filled > 0.5, rows, EMPTY).astype(jnp.bfloat16)

    def to_owner(turn):
        docs, spot_side, _, slot = turn_target(turn)
        return pltpu.make_async_remote_copy(
            src_ref=packed_ref.at[turn],
            dst_ref=own_ref.at[slot],
            send_sem=pack_send.at[turn],
            recv_sem=pack_recv.at[slot],
            device_id={"docs": docs, "help": spot_side},
            device_id_type=pl.DeviceIdType.MESH,
        )

    def from_source(slot):
        return pltpu.make_async_remote_copy(
            src_ref=packed_ref.at[0],
            dst_ref=own_ref.at[slot],
            send_sem=pack_send.at[0],
            recv_sem=pack_recv.at[slot],
            device_id=peer_id(0, 1),
            device_id_type=pl.DeviceIdType.MESH,
        )

    my_number = (me - quarter) * 2 + side
    my_slot = near * 2 + side

    def back(number, position):
        where = peer_id(*peers[position])
        slot = (where["docs"] + my_half * (owners - 1 - 2 * where["docs"])) * 2 + where["help"]
        return pltpu.make_async_remote_copy(
            src_ref=maxima_ref.at[slot // group],
            dst_ref=returned_ref.at[number],
            send_sem=back_send.at[position],
            recv_sem=back_recv.at[number],
            device_id=where,
            device_id_type=pl.DeviceIdType.MESH,
        )

    for turn in range(owners):
        docs, spot_side, number, slot = turn_target(turn)
        remote = (docs != me) | (side != spot_side)
        packed_ref[turn] = pack(number)
        if turn == 0:
            await_greetings(barrier)
            greet(onward_sem)
        if turn == half:
            await_greetings(onward_sem)

        @pl.when(remote)
        def _():
            to_owner(turn).start()

        @pl.when(jnp.logical_not(remote))
        def _():
            own_ref[slot] = packed_ref[turn]

    def column_max(columns, rows, same):
        scores = lax.dot_general(
            columns, rows, (((1,), (1,)), ((), ())), preferred_element_type=jnp.float32
        )
        keep = columns[:, 0:1].astype(jnp.float32) < 1.5
        if same:
            keep = keep & (
                lax.broadcasted_iota(jnp.int32, scores.shape, 0)
                != lax.broadcasted_iota(jnp.int32, scores.shape, 1)
            )
        return jnp.max(jnp.where(keep, scores, -1.0), axis=0, keepdims=True)

    @pl.when(is_owner)
    def _():
        for slot in range(late):

            @pl.when(my_slot != slot)
            def _():
                from_source(slot).wait_recv()

        first = own_ref[:late].reshape(late * slot_cap, feat_dim)
        first_max = column_max(first, first, True)
        for slot in range(late, sources):
            from_source(slot).wait_recv()
        last = own_ref[late:].reshape((sources - late) * slot_cap, feat_dim)
        maxima = jnp.concatenate(
            [
                jnp.maximum(first_max, column_max(last, first, False)),
                jnp.maximum(column_max(first, last, False), column_max(last, last, True)),
            ],
            axis=1,
        )
        for part in range(sources // group):
            maxima_ref[part] = maxima[:, part * row_count : (part + 1) * row_count]
        for position in range(len(peers)):
            back(my_number, position).start()
        returned_ref[my_number] = maxima_ref[my_slot // group]

    owner_half = (dest // 2 + quarter) // half
    my_slots = jnp.where(owner_half == my_half, near, owners - 1 - near) * 2 + side
    finder = jnp.where(
        lax.broadcasted_iota(jnp.int32, (row_count, row_count), 0)
        == my_slots % group * slot_cap + rank,
        1.0,
        0.0,
    ).astype(jnp.bfloat16)
    for number in range(owners):

        @pl.when((my_number != number) | jnp.logical_not(is_owner))
        def _():
            back(number, 0).wait_recv()

    exact = jnp.concatenate([returned_ref[number] for number in range(owners)], axis=0)
    parts = []
    for _ in range(3):
        part = exact.astype(jnp.bfloat16)
        parts.append(part.astype(jnp.float32))
        exact = exact - parts[-1]
    picked = jnp.dot(
        jnp.concatenate(parts, axis=0).astype(jnp.bfloat16),
        finder,
        preferred_element_type=jnp.float32,
    )
    picked = picked[:owners] + (picked[owners : 2 * owners] + picked[2 * owners :])
    mine = lax.broadcasted_iota(jnp.int32, picked.shape, 0) == dest
    out_ref[...] = jnp.sum(jnp.where(mine, picked, 0.0), axis=0, keepdims=True)
    for turn in range(owners):
        docs, spot_side, _, _ = turn_target(turn)

        @pl.when((docs != me) | (side != spot_side))
        def _():
            to_owner(turn).wait_send()

    @pl.when(is_owner)
    def _():
        for position in range(len(peers)):
            back(my_number, position).wait_send()


def fused_body(token_states, lengths, cluster_id, proj_weight, proj_bias):
    row_count, seq_len, feat_dim = token_states.shape
    owners = lax.axis_size("docs")
    slot_cap = 2 * row_count // owners
    vmem = pl.BlockSpec(memory_space=pltpu.VMEM)
    hbm = pl.BlockSpec(memory_space=pl.ANY)
    sources = 2 * owners
    result = pl.pallas_call(
        functools.partial(fused_kernel, owners, slot_cap),
        out_shape=jax.ShapeDtypeStruct((1, row_count), jnp.float32),
        in_specs=[hbm, vmem, vmem, hbm, vmem],
        out_specs=vmem,
        scratch_shapes=[
            pltpu.VMEM(token_states.shape, jnp.bfloat16),
            pltpu.VMEM(proj_weight.shape, jnp.bfloat16),
            pltpu.VMEM((owners, slot_cap, feat_dim), jnp.bfloat16),
            pltpu.VMEM((sources, slot_cap, feat_dim), jnp.bfloat16),
            pltpu.VMEM((sources * slot_cap // row_count, 1, row_count), jnp.float32),
            pltpu.VMEM((owners, 1, row_count), jnp.float32),
            pltpu.SemaphoreType.DMA,
            pltpu.SemaphoreType.DMA,
            pltpu.SemaphoreType.DMA((owners,)),
            pltpu.SemaphoreType.DMA((sources,)),
            pltpu.SemaphoreType.DMA((sources,)),
            pltpu.SemaphoreType.DMA((owners,)),
            pltpu.SemaphoreType.REGULAR,
        ],
        compiler_params=pltpu.CompilerParams(collective_id=0, has_side_effects=True),
        name="scores",
    )(token_states, lengths[None, :], cluster_id[None, :], proj_weight, proj_bias[None, :])
    return result.reshape(row_count)


def solution(mesh):
    in_specs = (
        P(("groups", "docs", "help"), None, None),
        P(("groups", "docs", "help")),
        P(("groups", "docs", "help")),
        P(),
        P(),
    )
    out_specs = P(("groups", "docs", "help"))
    owners = mesh.shape["docs"]
    direct = 8 <= owners <= DIRECT_LIMIT and owners & (owners - 1) == 0 and mesh.shape["help"] == 2
    return jax.shard_map(fused_body if direct else body, mesh=mesh, in_specs=in_specs, out_specs=out_specs, check_vma=False)
```

```python
import functools

import jax
import jax.numpy as jnp
from jax import lax
from jax.experimental import pallas as pl
from jax.experimental.pallas import tpu as pltpu
from jax.sharding import PartitionSpec as P

CL_OWN = 1


def partner(value, axis, bit):
    return lax.ppermute(value, axis, [(i, i ^ 1 << bit) for i in range(lax.axis_size(axis))])


def slot_maxima(own_emb, own_ids, self_pos, col_emb, col_ids):
    row_total = own_emb.shape[0]
    block = min(row_total, 512)
    col_pos = lax.broadcasted_iota(jnp.int32, (col_emb.shape[0],), 0)

    def block_max(pieces):
        part_emb, part_ids, part_self = pieces
        duplicate_scores = jnp.einsum(
            "rd,cd->rc", part_emb, col_emb, preferred_element_type=jnp.float32
        )
        match = (
            (part_ids[:, None] == col_ids[None, :])
            & (col_ids[None, :] >= 0)
            & (part_self[:, None] != col_pos[None, :])
        )
        return jnp.max(jnp.where(match, duplicate_scores, -1.0), axis=1)

    steps_count = row_total // block
    result = lax.map(
        block_max,
        (
            own_emb.reshape(steps_count, block, own_emb.shape[1]),
            own_ids.reshape(steps_count, block),
            self_pos.reshape(steps_count, block),
        ),
    )
    return result.reshape(row_total)


def body(token_states, lengths, cluster_id, proj_weight, proj_bias):
    row_count, seq_len, feat_dim = token_states.shape
    owners = lax.axis_size("docs")
    slot_cap = 2 * row_count // owners
    position_count = owners * slot_cap
    token_mask = (
        lax.broadcasted_iota(jnp.int32, (row_count, seq_len), 1) < lengths[:, None]
    ).astype(jnp.bfloat16)
    summed = jnp.einsum("rsd,rs->rd", token_states, token_mask, preferred_element_type=jnp.float32)
    pooled = (summed / lengths[:, None].astype(jnp.float32)).astype(jnp.bfloat16)
    hidden = jnp.tanh(jnp.dot(pooled, proj_weight, preferred_element_type=jnp.float32) + proj_bias)
    factor = lax.rsqrt(jnp.sum(hidden * hidden, axis=1, keepdims=True) + 1e-06)
    embedded = (hidden * factor).astype(jnp.bfloat16)
    dest_owner = cluster_id // CL_OWN
    same_owner = dest_owner[:, None] == dest_owner[None, :]
    earlier = lax.broadcasted_iota(jnp.int32, (row_count, row_count), 1) < lax.broadcasted_iota(
        jnp.int32, (row_count, row_count), 0
    )
    slot_rank = jnp.sum((same_owner & earlier).astype(jnp.int32), axis=1)
    target = dest_owner * slot_cap + slot_rank
    chooser = lax.broadcasted_iota(jnp.int32, (position_count, row_count), 0) == target[None, :]
    packed = jnp.dot(
        chooser.astype(jnp.bfloat16), embedded, preferred_element_type=jnp.float32
    ).astype(jnp.bfloat16)
    packed_ids = jnp.max(jnp.where(chooser, cluster_id[None, :], -1), axis=1)
    own_emb, own_ids = (
        lax.all_to_all(packed, "docs", split_axis=0, concat_axis=0, tiled=True),
        lax.all_to_all(packed_ids, "docs", split_axis=0, concat_axis=0, tiled=True),
    )
    mate_emb, mate_ids = partner((own_emb, own_ids), "help", 0)
    col_emb = jnp.concatenate([own_emb, mate_emb], axis=0)
    col_ids = jnp.concatenate([own_ids, mate_ids], axis=0)
    self_pos = lax.broadcasted_iota(jnp.int32, (position_count,), 0)
    maxima = slot_maxima(own_emb, own_ids, self_pos, col_emb, col_ids)
    returned = lax.all_to_all(maxima, "docs", split_axis=0, concat_axis=0, tiled=True)
    return jnp.max(jnp.where(chooser, returned[:, None], -3.0), axis=0)


EMPTY = 2.0
DIRECT_LIMIT = 16


def flipped(index, step):
    bit = 1
    while bit <= step:
        if step & bit:
            index = index + bit * (1 - 2 * ((index // bit) % 2))
        bit *= 2
    return index


def fused_kernel(
    owners,
    slot_cap,
    states_hbm,
    lengths_hbm,
    ids_hbm,
    weight_hbm,
    bias_hbm,
    out_ref,
    lengths_ref,
    ids_ref,
    bias_ref,
    states_ref,
    weight_ref,
    packed_ref,
    own_ref,
    maxima_ref,
    returned_ref,
    small_sem,
    states_sem,
    weight_sem,
    pack_send,
    pack_recv,
    back_send,
    back_recv,
    onward_sem,
):
    me = lax.axis_index("docs")
    side = lax.axis_index("help")
    row_count, seq_len, feat_dim = states_ref.shape
    quarter = owners // 4
    half = owners // 2
    sources = 2 * owners
    late = 2 * 3 * quarter
    group = row_count // slot_cap
    my_half = me // half
    near = me + my_half * (owners - 1 - 2 * me)
    outer = 1 - near // quarter
    is_owner = near >= quarter

    small_copies = [
        pltpu.make_async_copy(source, held, small_sem.at[position])
        for position, (source, held) in enumerate(
            [(ids_hbm, ids_ref), (lengths_hbm, lengths_ref), (bias_hbm, bias_ref)]
        )
    ]
    for copy in small_copies:
        copy.start()
    states_copy = pltpu.make_async_copy(states_hbm, states_ref, states_sem)
    states_copy.start()
    weight_copy = pltpu.make_async_copy(weight_hbm, weight_ref, weight_sem)
    weight_copy.start()
    barrier = pltpu.get_barrier_semaphore()
    peers = [(step, flip) for step in range(owners - 1, -1, -1) for flip in (0, 1) if step + flip]

    def peer_id(step, flip):
        return {"docs": flipped(me, step), "help": flipped(side, flip)}

    inner = [(spot, spot_side) for spot in range(quarter, half) for spot_side in (0, 1)]

    def greet(semaphore):
        def signal(spot, spot_side):
            docs = spot + my_half * (owners - 1 - 2 * spot)
            pl.semaphore_signal(
                semaphore,
                inc=1,
                device_id={"docs": docs, "help": spot_side},
                device_id_type=pl.DeviceIdType.MESH,
            )

        @pl.when(is_owner)
        def _():
            for spot, spot_side in inner:
                signal(owners - 1 - spot, spot_side)
                signal(spot - quarter, spot_side)

        @pl.when(jnp.logical_not(is_owner))
        def _():
            for spot, spot_side in inner:
                signal(spot, spot_side)

    def await_greetings(semaphore):
        pl.semaphore_wait(semaphore, len(inner) * (2 - outer))

    greet(barrier)

    for copy in small_copies:
        copy.wait()
    ids = ids_ref[...]
    across = jnp.broadcast_to(ids, (row_count, row_count))
    down = jnp.transpose(across)
    earlier = lax.broadcasted_iota(jnp.int32, (row_count, row_count), 0) < lax.broadcasted_iota(
        jnp.int32, (row_count, row_count), 1
    )
    rank = jnp.sum(jnp.where((across == down) & earlier, 1, 0), axis=0, keepdims=True)
    dest = ids // CL_OWN

    counts = jnp.transpose(
        jnp.broadcast_to(lengths_ref[...].astype(jnp.float32), (row_count, row_count))
    )[:, 0:1]
    states_copy.wait()
    states = states_ref[...]
    summed = states[:, 0, :].astype(jnp.float32)
    for position in range(1, seq_len):
        token = states[:, position, :].astype(jnp.float32)
        summed = summed + jnp.where(counts > position, token, 0.0)
    pooled = (summed / counts).astype(jnp.bfloat16)

    weight_copy.wait()
    hidden = jnp.tanh(
        jnp.dot(pooled, weight_ref[...], preferred_element_type=jnp.float32) + bias_ref[...]
    )
    factor = lax.rsqrt(jnp.sum(hidden * hidden, axis=1, keepdims=True) + 1e-06)
    embedded = (hidden * factor).astype(jnp.bfloat16)

    def turn_target(turn):
        spot = quarter + (turn // 2 + (1 - outer) * quarter) % half
        spot_side = turn % 2
        docs = spot + my_half * (owners - 1 - 2 * spot)
        number = (docs - quarter) * 2 + spot_side
        crosses = spot // half
        slot = (near + crosses * (owners - 1 - 2 * near)) * 2 + side
        return docs, spot_side, number, slot

    def pack(number):
        slots = lax.broadcasted_iota(jnp.int32, (slot_cap, row_count), 0)
        chooser = jnp.where((slots == rank) & (dest == number), 1.0, 0.0)
        filled = jnp.sum(chooser, axis=1, keepdims=True)
        rows = jnp.dot(
            chooser.astype(jnp.bfloat16), embedded, preferred_element_type=jnp.float32
        )
        return jnp.where(filled > 0.5, rows, EMPTY).astype(jnp.bfloat16)

    def to_owner(turn):
        docs, spot_side, _, slot = turn_target(turn)
        return pltpu.make_async_remote_copy(
            src_ref=packed_ref.at[turn],
            dst_ref=own_ref.at[slot],
            send_sem=pack_send.at[turn],
            recv_sem=pack_recv.at[slot],
            device_id={"docs": docs, "help": spot_side},
            device_id_type=pl.DeviceIdType.MESH,
        )

    def from_source(slot):
        return pltpu.make_async_remote_copy(
            src_ref=packed_ref.at[0],
            dst_ref=own_ref.at[slot],
            send_sem=pack_send.at[0],
            recv_sem=pack_recv.at[slot],
            device_id=peer_id(0, 1),
            device_id_type=pl.DeviceIdType.MESH,
        )

    my_number = (me - quarter) * 2 + side
    my_slot = near * 2 + side

    def back(number, position):
        where = peer_id(*peers[position])
        slot = (where["docs"] + my_half * (owners - 1 - 2 * where["docs"])) * 2 + where["help"]
        return pltpu.make_async_remote_copy(
            src_ref=maxima_ref.at[slot // group],
            dst_ref=returned_ref.at[number],
            send_sem=back_send.at[position],
            recv_sem=back_recv.at[number],
            device_id=where,
            device_id_type=pl.DeviceIdType.MESH,
        )

    for turn in range(owners):
        docs, spot_side, number, slot = turn_target(turn)
        remote = (docs != me) | (side != spot_side)
        packed_ref[turn] = pack(number)
        if turn == 0:
            await_greetings(barrier)
            greet(onward_sem)
        if turn == half:
            await_greetings(onward_sem)

        @pl.when(remote)
        def _():
            to_owner(turn).start()

        @pl.when(jnp.logical_not(remote))
        def _():
            own_ref[slot] = packed_ref[turn]

    def column_max(columns, rows, same):
        scores = lax.dot_general(
            columns, rows, (((1,), (1,)), ((), ())), preferred_element_type=jnp.float32
        )
        keep = columns[:, 0:1].astype(jnp.float32) < 1.5
        if same:
            keep = keep & (
                lax.broadcasted_iota(jnp.int32, scores.shape, 0)
                != lax.broadcasted_iota(jnp.int32, scores.shape, 1)
            )
        return jnp.max(jnp.where(keep, scores, -1.0), axis=0, keepdims=True)

    @pl.when(is_owner)
    def _():
        for slot in range(late):

            @pl.when(my_slot != slot)
            def _():
                from_source(slot).wait_recv()

        first = own_ref[:late].reshape(late * slot_cap, feat_dim)
        first_max = column_max(first, first, True)
        for slot in range(late, sources):
            from_source(slot).wait_recv()
        last = own_ref[late:].reshape((sources - late) * slot_cap, feat_dim)
        maxima = jnp.concatenate(
            [
                jnp.maximum(first_max, column_max(last, first, False)),
                jnp.maximum(column_max(first, last, False), column_max(last, last, True)),
            ],
            axis=1,
        )
        for part in range(sources // group):
            maxima_ref[part] = maxima[:, part * row_count : (part + 1) * row_count]
        for position in range(len(peers)):
            back(my_number, position).start()
        returned_ref[my_number] = maxima_ref[my_slot // group]

    owner_half = (dest // 2 + quarter) // half
    my_slots = jnp.where(owner_half == my_half, near, owners - 1 - near) * 2 + side
    finder = jnp.where(
        lax.broadcasted_iota(jnp.int32, (row_count, row_count), 0)
        == my_slots % group * slot_cap + rank,
        1.0,
        0.0,
    ).astype(jnp.bfloat16)
    for number in range(owners):

        @pl.when((my_number != number) | jnp.logical_not(is_owner))
        def _():
            back(number, 0).wait_recv()

    exact = jnp.concatenate([returned_ref[number] for number in range(owners)], axis=0)
    parts = []
    for _ in range(3):
        part = exact.astype(jnp.bfloat16)
        parts.append(part.astype(jnp.float32))
        exact = exact - parts[-1]
    picked = jnp.dot(
        jnp.concatenate(parts, axis=0).astype(jnp.bfloat16),
        finder,
        preferred_element_type=jnp.float32,
    )
    picked = picked[:owners] + (picked[owners : 2 * owners] + picked[2 * owners :])
    mine = lax.broadcasted_iota(jnp.int32, picked.shape, 0) == dest
    out_ref[...] = jnp.sum(jnp.where(mine, picked, 0.0), axis=0, keepdims=True)
    for turn in range(owners):
        docs, spot_side, _, _ = turn_target(turn)

        @pl.when((docs != me) | (side != spot_side))
        def _():
            to_owner(turn).wait_send()

    @pl.when(is_owner)
    def _():
        for position in range(len(peers)):
            back(my_number, position).wait_send()


def fused_body(token_states, lengths, cluster_id, proj_weight, proj_bias):
    row_count, seq_len, feat_dim = token_states.shape
    owners = lax.axis_size("docs")
    slot_cap = 2 * row_count // owners
    vmem = pl.BlockSpec(memory_space=pltpu.VMEM)
    hbm = pl.BlockSpec(memory_space=pl.ANY)
    sources = 2 * owners
    result = pl.pallas_call(
        functools.partial(fused_kernel, owners, slot_cap),
        out_shape=pltpu.VMEM((1, row_count), jnp.float32),
        in_specs=[hbm] * 5,
        out_specs=vmem,
        scratch_shapes=[
            pltpu.VMEM((1, row_count), jnp.int32),
            pltpu.VMEM((1, row_count), jnp.int32),
            pltpu.VMEM((1, feat_dim), jnp.float32),
            pltpu.VMEM(token_states.shape, jnp.bfloat16),
            pltpu.VMEM(proj_weight.shape, jnp.bfloat16),
            pltpu.VMEM((owners, slot_cap, feat_dim), jnp.bfloat16),
            pltpu.VMEM((sources, slot_cap, feat_dim), jnp.bfloat16),
            pltpu.VMEM((sources * slot_cap // row_count, 1, row_count), jnp.float32),
            pltpu.VMEM((owners, 1, row_count), jnp.float32),
            pltpu.SemaphoreType.DMA((3,)),
            pltpu.SemaphoreType.DMA,
            pltpu.SemaphoreType.DMA,
            pltpu.SemaphoreType.DMA((owners,)),
            pltpu.SemaphoreType.DMA((sources,)),
            pltpu.SemaphoreType.DMA((sources,)),
            pltpu.SemaphoreType.DMA((owners,)),
            pltpu.SemaphoreType.REGULAR,
        ],
        compiler_params=pltpu.CompilerParams(collective_id=0, has_side_effects=True),
        name="scores",
    )(token_states, lengths[None, :], cluster_id[None, :], proj_weight, proj_bias[None, :])
    return result.reshape(row_count)


def solution(mesh):
    in_specs = (
        P(("groups", "docs", "help"), None, None),
        P(("groups", "docs", "help")),
        P(("groups", "docs", "help")),
        P(),
        P(),
    )
    out_specs = P(("groups", "docs", "help"))
    owners = mesh.shape["docs"]
    direct = 8 <= owners <= DIRECT_LIMIT and owners & (owners - 1) == 0 and mesh.shape["help"] == 2
    return jax.shard_map(fused_body if direct else body, mesh=mesh, in_specs=in_specs, out_specs=out_specs, check_vma=False)
```
